32 devices in a mesh: groups: 2 (over x), shard: 16 (over z, y, core).
Axes of the slice: x: 2, y: 2, z: 4, core: 2. Of those that a mesh axis runs over, the one named last changes fastest.
Arguments:
- residual_in: bfloat16 [128, 5120], P('groups', 'shard'), parts along dimension 0, may hold values from -12 to 12
- queries: bfloat16 [64, 16, 640], P(('groups', 'shard')), parts along dimension 0, may hold values from -8 to 8
- key_cache: bfloat16 [64, 4096, 128], P(('groups', 'shard')), parts along dimension 0, may hold values from -6 to 6
- value_cache: bfloat16 [64, 4096, 128], P(('groups', 'shard')), parts along dimension 0, may hold values from -6 to 6
- new_keys: bfloat16 [64, 16, 128], P(('groups', 'shard')), parts along dimension 0, may hold values from -8 to 8
- new_values: bfloat16 [64, 16, 128], P(('groups', 'shard')), parts along dimension 0, may hold values from -6 to 6
- cache_len: int32 [8], P('groups'), parts along dimension 0, may hold values from 1024 to 4096, as said below
- tree_mask: int32 [8, 16, 16], P('groups'), parts along dimension 0, may hold values from 0 to 1, as said below
- out_proj: bfloat16 [5120, 5120], P(None, 'shard'), may hold values from -0.25 to 0.25
- norm_gain: bfloat16 [5120], P('shard'), may hold values from 0.099609375 to 1.8984375
- gate_w: bfloat16 [5120, 27648], P(None, 'shard'), may hold values from -0.078125 to 0.078125
- up_w: bfloat16 [5120, 27648], P(None, 'shard'), may hold values from -0.078125 to 0.078125
- down_w: bfloat16 [27648, 5120], P('shard'), may hold values from -0.0390625 to 0.0390625
Outputs:
- layer_out: bfloat16 [128, 5120], P(('groups', 'shard')), parts along dimension 0
The draws below stay inside these ranges and needn't reach their ends.
There are 2 independent parts, one for each index of `groups`. The reference program is written for one: setup_inputs(seed, part) draws one part's arguments, and reference() takes and returns one part's arrays. A program takes and returns all parts, laid end to end along the dimension named above; an argument that names none is the same for every part. Nothing has to cross between parts.
Inputs may be any that keep to these rules, and one draw needn't show every extreme that they name: Positions 0 to cache_len[r] - 1 of request r's blocks are valid; some request fills all 4096 positions. tree_mask[r, i, j] is 1 exactly where draft row j is row i itself or an ancestor of row i in request r's draft tree; a row's parent comes before it, and row 0 is the root.
All inputs are finite; a program needn't handle non-finite values.
Results may differ from the reference program's by a relative error of at most 0.0059.
Values may be sent and summed in bfloat16 or wider, within the bound.
No kernel may reach another device: no remote copies, remote signals or barrier semaphores. Data moves between devices by JAX's collectives and lax.ppermute only.
A program may use at most 128 MiB of HBM per device.

```python
import math
import jax
import jax.numpy as jnp
from jax import lax

D = 5120
FF = 27648
HQ = 40
KV = 8
HD = 128
L = 4096
DR = 16
G = 5
PAIRS = 32
REQ = 4
ROWS = 64


def draw_residual_in(key, part):
    column_pos = jnp.arange(D, dtype=jnp.float32) / D
    jitter = jax.random.uniform(jax.random.fold_in(key, 11), (D,), jnp.float32, 0.7, 1.4)
    column_scale = 0.5 * jnp.power(3.0, column_pos) * jitter
    values = jax.random.normal(jax.random.fold_in(key, 12), (ROWS, D), jnp.float32) * column_scale[None, :]
    return jnp.clip(values, -12.0, 12.0).astype(jnp.bfloat16)


def draw_queries(key, part):
    values = jnp.clip(2.0 * jax.random.normal(jax.random.fold_in(key, 21), (PAIRS, DR, G * HD), jnp.float32), -8.0, 8.0)
    return values.astype(jnp.bfloat16)


def draw_key_cache(key, part):
    values = jnp.clip(jax.random.normal(jax.random.fold_in(key, 22), (PAIRS, L, HD), jnp.float32), -6.0, 6.0)
    return values.astype(jnp.bfloat16)


def draw_cache_len(key, part):
    lengths = jax.random.randint(jax.random.fold_in(key, 31), (REQ,), L // 4, L + 1)
    selected_entry = jax.random.randint(jax.random.fold_in(key, 32), (), 0, REQ)
    return jnp.where(jnp.arange(REQ, dtype=jnp.int32) == selected_entry, L, lengths).astype(jnp.int32)


def draw_tree_mask(key, part):
    positions = jnp.arange(DR, dtype=jnp.int32)
    parent = jax.random.randint(jax.random.fold_in(key, 41), (REQ, DR), 0, jnp.maximum(positions, 1)[None, :])
    parent_link = ((parent[:, :, None] == positions[None, None, :]) & (positions[None, :, None] > 0)).astype(jnp.int32)
    identity = jnp.broadcast_to(jnp.eye(DR, dtype=jnp.int32), (REQ, DR, DR))
    reached = identity
    current = identity
    for repeat_factor in range(DR):
        current = jnp.minimum(jnp.einsum('rij,rjk->rik', current, parent_link), 1)
        reached = jnp.maximum(reached, current)
    return reached.astype(jnp.int32)


def level_of(rng, dims, split, low, high):
    factor_of, own = 1.0, jax.random.fold_in(rng, 6)
    for dim, shards_of in split:
        draws = jnp.exp(jax.random.uniform(jax.random.fold_in(own, dim), (shards_of,), jnp.float32, low / len(split), high / len(split)))
        factor_of = factor_of * jnp.repeat(draws, dims[dim] // shards_of).reshape([-1 if axis == dim else 1 for axis in range(len(dims))])
    return factor_of


def centred(key, shape, deviation, most, shards=(), kind=jnp.bfloat16):
    factor_of = level_of(key, shape, shards, -0.22, 0.18) if shards else 1.0
    values = jax.random.normal(key, shape, jnp.float32) * deviation * factor_of
    return jnp.minimum(jnp.maximum(values, -most), most).astype(kind)


def setup_inputs(seed: int = 0, part: int = 0) -> dict:
    keys = jax.random.split(jax.random.key(seed), 14)
    part_splits = jax.random.split(jax.random.fold_in(keys[13], part), 14)
    residual_in = draw_residual_in(jax.random.fold_in(jax.random.fold_in(keys[13], part), 71), part)
    queries = draw_queries(jax.random.fold_in(jax.random.fold_in(keys[13], part), 71), part)
    key_cache = draw_key_cache(jax.random.fold_in(jax.random.fold_in(keys[13], part), 71), part)
    value_cache = centred(part_splits[3], (PAIRS, L, HD), 1.0, 6.0, ((0, 16),))
    new_keys = centred(part_splits[4], (PAIRS, DR, HD), 2.0, 8.0, ((0, 16),))
    new_values = centred(part_splits[5], (PAIRS, DR, HD), 1.0, 6.0, ((0, 16),))
    cache_len = draw_cache_len(jax.random.fold_in(jax.random.fold_in(keys[13], part), 71), part)
    tree_mask = draw_tree_mask(jax.random.fold_in(jax.random.fold_in(keys[13], part), 71), part)
    out_proj = centred(keys[8], (HQ * HD, D), (G * HD) ** -0.5, 0.25, ((1, 16),))
    norm_gain = jnp.clip(1.0 + 0.18 * jax.random.normal(keys[9], (D,), jnp.float32), 0.099609375, 1.8984375).astype(jnp.bfloat16)
    gate_w = centred(keys[10], (D, FF), D ** -0.5, 0.078125, ((1, 16),))
    up_w = centred(keys[11], (D, FF), D ** -0.5, 0.078125, ((1, 16),))
    down_w = centred(keys[12], (FF, D), FF ** -0.5, 0.0390625, ((0, 16),))
    return {"residual_in": residual_in, "queries": queries, "key_cache": key_cache, "value_cache": value_cache, "new_keys": new_keys, "new_values": new_values, "cache_len": cache_len, "tree_mask": tree_mask, "out_proj": out_proj, "norm_gain": norm_gain, "gate_w": gate_w, "up_w": up_w, "down_w": down_w}


def attend_pair(query_matrix, cache_keys, cache_values, draft_keys, draft_values, length, tree):
    head_rows = query_matrix.astype(jnp.float32).reshape(DR, G, HD)
    score_scale = 1.0 / math.sqrt(HD)
    cache_scores = jnp.einsum('dgk,lk->dgl', head_rows, cache_keys.astype(jnp.float32)) * score_scale
    draft_scores = jnp.einsum('dgk,ek->dge', head_rows, draft_keys.astype(jnp.float32)) * score_scale
    valid_keys = jnp.arange(L, dtype=jnp.int32) < length
    cache_scores = jnp.where(valid_keys[None, None, :], cache_scores, -1e+30)
    draft_scores = jnp.where(tree[:, None, :] > 0, draft_scores, -1e+30)
    peak_score = jnp.maximum(lax.optimization_barrier(jnp.max(cache_scores, axis=-1)), lax.optimization_barrier(jnp.max(draft_scores, axis=-1)))
    cache_weights = jnp.where(valid_keys[None, None, :], jnp.exp(cache_scores - peak_score[..., None]), 0.0)
    draft_weights = jnp.where(tree[:, None, :] > 0, jnp.exp(draft_scores - peak_score[..., None]), 0.0)
    denom = lax.optimization_barrier(jnp.sum(cache_weights, axis=-1)) + lax.optimization_barrier(jnp.sum(draft_weights, axis=-1))
    cache_low = cache_weights.astype(jnp.bfloat16).astype(jnp.float32)
    draft_low = draft_weights.astype(jnp.bfloat16).astype(jnp.float32)
    weighted = jnp.einsum('dgl,lk->dgk', cache_low, cache_values.astype(jnp.float32))
    weighted = weighted + jnp.einsum('dge,ek->dgk', draft_low, draft_values.astype(jnp.float32))
    return (weighted / denom[..., None]).astype(jnp.bfloat16).reshape(DR, G * HD)

def reference(residual_in, queries, key_cache, value_cache, new_keys, new_values, cache_len, tree_mask, out_proj, norm_gain, gate_w, up_w, down_w):

    def one_pair(pair):
        request = pair % REQ
        return attend_pair(queries[pair], key_cache[pair], value_cache[pair], new_keys[pair], new_values[pair], cache_len[request], tree_mask[request])
    attn = lax.map(one_pair, jnp.arange(PAIRS, dtype=jnp.int32))
    grouped = attn.astype(jnp.float32).reshape(KV, REQ, DR, G * HD)
    head_projection = out_proj.astype(jnp.float32).reshape(KV, G * HD, D)
    mixed = jnp.einsum('hrdf,hfc->rdc', grouped, head_projection).reshape(ROWS, D)
    stream = (residual_in.astype(jnp.float32) + mixed).astype(jnp.bfloat16)
    wide_rows = stream.astype(jnp.float32)
    squares = lax.optimization_barrier(jnp.sum(wide_rows * wide_rows, axis=1))
    inverse = lax.rsqrt(squares / D + 1e-06)
    normed = (wide_rows * inverse[:, None] * norm_gain.astype(jnp.float32)[None, :]).astype(jnp.bfloat16)
    gate_acts = jnp.dot(normed, gate_w, preferred_element_type=jnp.float32)
    up_acts = jnp.dot(normed, up_w, preferred_element_type=jnp.float32)
    hidden = (jax.nn.silu(gate_acts) * up_acts).astype(jnp.bfloat16)
    summed = jnp.dot(hidden, down_w, preferred_element_type=jnp.float32)
    return (wide_rows + summed).astype(jnp.bfloat16)
```

```python
import functools
import math

import jax
import jax.numpy as jnp
from jax import lax
from jax.experimental import pallas as pl
from jax.experimental.pallas import tpu as pltpu
from jax.sharding import PartitionSpec as P

D = 5120
KV = 8
HD = 128
G = 5
F32 = jnp.float32
BF16 = jnp.bfloat16
LANES = 128


def attention(queries, key_cache, value_cache, new_keys, new_values, cache_len, tree_mask):
    blocks = queries.shape[0]
    drafts = queries.shape[1]
    requests = cache_len.shape[0]
    first_pair = lax.axis_index("shard") * blocks
    pair_index = first_pair + jnp.arange(blocks, dtype=jnp.int32)
    req_index = pair_index % requests
    lengths = cache_len[req_index]
    tree_rows = tree_mask[req_index]
    head_rows = queries.reshape(blocks, drafts, G, HD)
    score_scale = 1.0 / math.sqrt(HD)
    cache_scores = (
        jnp.einsum("bdgk,blk->bdgl", head_rows, key_cache, preferred_element_type=F32)
        * score_scale
    )
    draft_scores = (
        jnp.einsum("bdgk,bek->bdge", head_rows, new_keys, preferred_element_type=F32)
        * score_scale
    )
    valid_keys = jnp.arange(key_cache.shape[1], dtype=jnp.int32)[None, :] < lengths[:, None]
    cache_scores = jnp.where(valid_keys[:, None, None, :], cache_scores, -1e30)
    draft_scores = jnp.where(tree_rows[:, :, None, :] > 0, draft_scores, -1e30)
    peak_score = jnp.maximum(jnp.max(cache_scores, axis=-1), jnp.max(draft_scores, axis=-1))
    cache_weights = jnp.where(
        valid_keys[:, None, None, :], jnp.exp(cache_scores - peak_score[..., None]), 0.0
    )
    draft_weights = jnp.where(
        tree_rows[:, :, None, :] > 0, jnp.exp(draft_scores - peak_score[..., None]), 0.0
    )
    denom = jnp.sum(cache_weights, axis=-1) + jnp.sum(draft_weights, axis=-1)
    weighted = jnp.einsum(
        "bdgl,blk->bdgk", cache_weights.astype(BF16), value_cache, preferred_element_type=F32
    )
    weighted = weighted + jnp.einsum(
        "bdge,bek->bdgk", draft_weights.astype(BF16), new_values, preferred_element_type=F32
    )
    attn = (weighted / denom[..., None]).astype(BF16)
    return attn.reshape(blocks * drafts, G * HD)


def swap(x, bit, size):
    return lax.ppermute(x, "shard", [(i, i ^ bit) for i in range(size)])


def gather(x, size):
    held = x[None]
    bit = size // 2
    while bit:
        held = jnp.concatenate([held, swap(held, bit, size)], axis=0)
        bit //= 2
    return held


def reversed_bits(value, size):
    out = jnp.zeros_like(value)
    low, high = 1, size // 2
    while high:
        out = out + jnp.where((value & low) > 0, high, 0)
        low *= 2
        high //= 2
    return out


def project_kernel(slot_ref, held_ref, w_ref, res_ref, gain_ref, out_ref, rows_ref, acc_ref, *, per_head):
    step = pl.program_id(0)
    high = held_ref.shape[1]

    @pl.when(step == 0)
    def _():
        acc_ref[...] = jnp.zeros_like(acc_ref)

    width = held_ref.shape[2]
    for part in range(w_ref.shape[0] // width):
        head = step * (w_ref.shape[0] // width) + part
        for i in range(per_head):
            rows_ref[i * high : (i + 1) * high, :] = held_ref[slot_ref[head * per_head + i]]
        acc_ref[...] += jnp.dot(
            rows_ref[...], w_ref[part * width : (part + 1) * width, :], preferred_element_type=F32
        )

    @pl.when(step == pl.num_programs(0) - 1)
    def _():
        stream = (res_ref[...].astype(F32) + acc_ref[...]).astype(BF16)
        cols = stream.shape[1]
        out_ref[:, :cols] = stream
        out_ref[:, cols:] = gain_ref[...]


def project(slots, held, out_proj, residual, gain_cols, per_head, heads_per_step):
    rows, cols = residual.shape
    wide = cols + gain_cols.shape[1]
    width = held.shape[2]
    steps = out_proj.shape[0] // (width * heads_per_step)
    whole = lambda *shape: pl.BlockSpec(shape, lambda i, s: (0,) * len(shape))
    return pl.pallas_call(
        functools.partial(project_kernel, per_head=per_head),
        grid_spec=pltpu.PrefetchScalarGridSpec(
            num_scalar_prefetch=1,
            grid=(steps,),
            in_specs=[
                whole(*held.shape),
                pl.BlockSpec((width * heads_per_step, cols), lambda i, s: (i, 0)),
                whole(*residual.shape),
                whole(*gain_cols.shape),
            ],
            out_specs=whole(rows, wide),
            scratch_shapes=[pltpu.VMEM((rows, width), BF16), pltpu.VMEM((rows, cols), F32)],
        ),
        out_shape=jax.ShapeDtypeStruct((rows, wide), BF16),
        name="project",
    )(slots, held, out_proj, residual, gain_cols)


def feed_kernel(slot_ref, held_ref, gate_ref, up_ref, order_ref, out_ref, norm_ref, gacc_ref, uacc_ref, *, cols, group):
    step = pl.program_id(0)
    rows = held_ref.shape[1]

    @pl.when(step == 0)
    def _():
        gacc_ref[...] = jnp.zeros_like(gacc_ref)
        uacc_ref[...] = jnp.zeros_like(uacc_ref)
        squares = jnp.zeros((rows, 1), F32)
        for j in range(held_ref.shape[0]):
            wide = held_ref[j][:, :cols].astype(F32)
            squares = squares + jnp.sum(wide * wide, axis=1, keepdims=True)
        inverse = lax.rsqrt(squares / (cols * held_ref.shape[0]) + 1e-06)
        spare = held_ref.shape[2] - cols
        pick = (
            lax.broadcasted_iota(jnp.int32, (spare, cols), 1) // rows
            == lax.broadcasted_iota(jnp.int32, (spare, cols), 0)
        ).astype(BF16)
        place = lax.broadcasted_iota(jnp.int32, (rows, cols), 1) % rows == lax.broadcasted_iota(
            jnp.int32, (rows, cols), 0
        )
        for t in range(held_ref.shape[0]):
            block = held_ref[slot_ref[t]]
            spread = jnp.dot(block[:, cols:], pick, preferred_element_type=F32)
            gain = jnp.sum(jnp.where(place, spread, 0.0), axis=0, keepdims=True)
            normed = (block[:, :cols].astype(F32) * inverse * gain).astype(BF16)
            norm_ref[t // group, :, (t % group) * cols : (t % group + 1) * cols] = normed

    x = norm_ref[step]
    gacc_ref[...] += jnp.dot(x, gate_ref[...], preferred_element_type=F32)
    uacc_ref[...] += jnp.dot(x, up_ref[...], preferred_element_type=F32)

    @pl.when(step == pl.num_programs(0) - 1)
    def _():
        gate = gacc_ref[...]
        hidden = (gate * jax.nn.sigmoid(gate) * uacc_ref[...]).astype(BF16)
        order = (
            order_ref[...] == lax.broadcasted_iota(jnp.int32, (rows, rows), 1)
        ).astype(BF16)
        out_ref[...] = jnp.dot(order, hidden, preferred_element_type=F32).astype(BF16)


def feed(slots, held, gate_w, up_w, order, cols, group):
    size, rows, wide = held.shape
    steps = size // group
    units = gate_w.shape[1]
    whole = lambda *shape: pl.BlockSpec(shape, lambda i, s: (0,) * len(shape))
    return pl.pallas_call(
        functools.partial(feed_kernel, cols=cols, group=group),
        grid_spec=pltpu.PrefetchScalarGridSpec(
            num_scalar_prefetch=1,
            grid=(steps,),
            in_specs=[
                whole(*held.shape),
                pl.BlockSpec((group * cols, units), lambda i, s: (i, 0)),
                pl.BlockSpec((group * cols, units), lambda i, s: (i, 0)),
                whole(*order.shape),
            ],
            out_specs=whole(rows, units),
            scratch_shapes=[
                pltpu.VMEM((steps, rows, group * cols), BF16),
                pltpu.VMEM((rows, units), F32),
                pltpu.VMEM((rows, units), F32),
            ],
        ),
        out_shape=jax.ShapeDtypeStruct((rows, units), BF16),
        name="feed",
    )(slots, held, gate_w, up_w, order)


def down_kernel(hidden_ref, w_ref, keep_ref, send_ref):
    term = jnp.dot(hidden_ref[...], w_ref[...], preferred_element_type=F32)
    half = term.shape[0] // 2
    keep_ref[...] = term[:half]
    send_ref[...] = term[half:].astype(BF16)


def down(hidden, down_w, tile):
    rows, units = hidden.shape
    width = down_w.shape[1]
    return pl.pallas_call(
        down_kernel,
        grid=(width // tile,),
        in_specs=[
            pl.BlockSpec((rows, units), lambda i: (0, 0)),
            pl.BlockSpec((units, tile), lambda i: (0, i)),
        ],
        out_specs=[
            pl.BlockSpec((rows // 2, tile), lambda i: (0, i)),
            pl.BlockSpec((rows // 2, tile), lambda i: (0, i)),
        ],
        out_shape=[
            jax.ShapeDtypeStruct((rows // 2, width), F32),
            jax.ShapeDtypeStruct((rows // 2, width), BF16),
        ],
        name="down",
    )(hidden, down_w)


def on_device(
    size,
    residual_in,
    queries,
    key_cache,
    value_cache,
    new_keys,
    new_values,
    cache_len,
    tree_mask,
    out_proj,
    norm_gain,
    gate_w,
    up_w,
    down_w,
):
    blocks, drafts = queries.shape[:2]
    requests = cache_len.shape[0]
    rows, cols = residual_in.shape
    own_rows = rows // size
    me = lax.axis_index("shard")
    devices = jnp.arange(size, dtype=jnp.int32)
    slots = reversed_bits(devices ^ me, size)
    order = (
        (me ^ reversed_bits(devices, size))[:, None] * own_rows
        + jnp.arange(own_rows, dtype=jnp.int32)[None, :]
    ).reshape(rows, 1)
    spare = -cols % LANES
    filled = -(-cols // rows)
    while spare < filled:
        spare += LANES
    gain_cols = jnp.pad(norm_gain, (0, filled * rows - cols)).reshape(filled, rows).T
    gain_cols = jnp.pad(gain_cols, ((0, 0), (0, spare - filled)))

    attn = attention(
        queries, key_cache, value_cache, new_keys, new_values, cache_len, tree_mask
    )
    held = gather(attn, size)
    payload = project(slots, held, out_proj, residual_in, gain_cols, requests // blocks, 2)
    held = gather(payload, size)
    group = size
    while group * cols > 640 and group > 1:
        group //= 2
    hidden = feed(slots, held, gate_w, up_w, order, cols, group)
    keep, send = down(hidden, down_w, 640)
    bit = 1
    while True:
        keep = keep + swap(send, bit, size).astype(F32)
        bit *= 2
        if bit == size:
            break
        half = keep.shape[0] // 2
        keep, send = keep[:half], keep[half:].astype(BF16)
    mine = lax.dynamic_slice_in_dim(held[:, :, :cols], me * own_rows, own_rows, axis=1)
    mine = mine[slots].transpose(1, 0, 2).reshape(own_rows, size * cols)
    return (mine.astype(F32) + keep).astype(BF16)


def solution(mesh):
    placed = (
        P("groups", "shard"),
        P(("groups", "shard"), None, None),
        P(("groups", "shard"), None, None),
        P(("groups", "shard"), None, None),
        P(("groups", "shard"), None, None),
        P(("groups", "shard"), None, None),
        P("groups"),
        P("groups", None, None),
        P(None, "shard"),
        P("shard"),
        P(None, "shard"),
        P(None, "shard"),
        P("shard", None),
    )
    return jax.shard_map(
        functools.partial(on_device, mesh.shape["shard"]),
        mesh=mesh,
        in_specs=placed,
        out_specs=P(("groups", "shard"), None),
        check_vma=False,
    )
```

```python
import functools
import math

import jax
import jax.numpy as jnp
from jax import lax
from jax.experimental import pallas as pl
from jax.experimental.pallas import tpu as pltpu
from jax.sharding import PartitionSpec as P

F32 = jnp.float32
BF16 = jnp.bfloat16
LANES = 128
MIB = 2**20
SPAN = 1024
HINT = pl.CostEstimate(flops=2 * 10**11, bytes_accessed=2 * 10**9, transcendentals=0)
IN_VMEM = pl.BlockSpec(memory_space=pltpu.VMEM)
IN_SMEM = pl.BlockSpec(memory_space=pltpu.SMEM)


def resident(x):
    return pltpu.with_memory_space_constraint(x, pltpu.VMEM)


def in_hbm(x):
    return pltpu.with_memory_space_constraint(x, pltpu.HBM)


def rows_dot(a, b):
    return lax.dot_general(a, b, (((1,), (1,)), ((), ())), preferred_element_type=F32)


def reversed_bits(value, size):
    out = value & 0
    low, high = 1, size // 2
    while high:
        out = out + ((value // low) % 2) * high
        low *= 2
        high //= 2
    return out


def traced_reversed_bits(value, size):
    out = value & 0
    low, high = 1, size // 2
    while high:
        out = jnp.where((value & low) != 0, out + high, out)
        low *= 2
        high //= 2
    return out


def swap(x, bit, size):
    return lax.ppermute(x, "shard", [(i, i ^ bit) for i in range(size)])


def gather(x, size):
    held = x[None]
    bit = size // 2
    while bit:
        held = jnp.concatenate([held, swap(held, bit, size)], axis=0)
        bit //= 2
    return held


def attend_kernel(me_ref, len_ref, q_ref, k_ref, v_ref, nk_ref, nv_ref, tree_ref, out_ref, *, heads, scale):
    block = pl.program_id(0)
    request = (me_ref[0] * pl.num_programs(0) + block) % tree_ref.shape[0]
    length = len_ref[request]
    drafts = q_ref.shape[1]
    width = k_ref.shape[2]
    q = jnp.concatenate([q_ref[0][:, g * width : (g + 1) * width] for g in range(heads)], axis=0)
    scores = rows_dot(q, k_ref[0]) * scale
    valid = lax.broadcasted_iota(jnp.int32, scores.shape, 1) < length
    scores = jnp.where(valid, scores, -1e30)
    fresh = rows_dot(q, nk_ref[0]) * scale
    seen = jnp.concatenate([tree_ref[request]] * heads, axis=0) > 0
    fresh = jnp.where(seen, fresh, -1e30)
    peak = jnp.maximum(
        jnp.max(scores, axis=1, keepdims=True), jnp.max(fresh, axis=1, keepdims=True)
    )
    weights = jnp.where(valid, jnp.exp(scores - peak), 0.0)
    fresh_weights = jnp.where(seen, jnp.exp(fresh - peak), 0.0)
    denom = jnp.sum(weights, axis=1, keepdims=True) + jnp.sum(fresh_weights, axis=1, keepdims=True)
    mixed = jnp.dot(weights.astype(BF16), v_ref[0], preferred_element_type=F32)
    mixed = mixed + jnp.dot(fresh_weights.astype(BF16), nv_ref[0], preferred_element_type=F32)
    attn = (mixed / denom).astype(BF16)
    for g in range(heads):
        out_ref[:, g * width : (g + 1) * width] = attn[g * drafts : (g + 1) * drafts]


def attend(me, queries, key_cache, value_cache, new_keys, new_values, cache_len, tree_mask):
    blocks, drafts, wide = queries.shape
    width = key_cache.shape[2]
    one = lambda x: pl.BlockSpec((1,) + x.shape[1:], lambda b, *_: (b, 0, 0))
    return pl.pallas_call(
        functools.partial(attend_kernel, heads=wide // width, scale=1.0 / math.sqrt(width)),
        grid_spec=pltpu.PrefetchScalarGridSpec(
            num_scalar_prefetch=2,
            grid=(blocks,),
            in_specs=[
                one(queries),
                one(key_cache),
                one(value_cache),
                one(new_keys),
                one(new_values),
                pl.BlockSpec(tree_mask.shape, lambda b, *_: (0, 0, 0)),
            ],
            out_specs=pl.BlockSpec((drafts, wide), lambda b, *_: (b, 0)),
        ),
        out_shape=jax.ShapeDtypeStruct((blocks * drafts, wide), BF16),
        compiler_params=pltpu.CompilerParams(vmem_limit_bytes=16 * MIB),
        cost_estimate=HINT,
        name="attend",
    )(me, cache_len, *map(in_hbm, (queries, key_cache, value_cache, new_keys, new_values, tree_mask)))


def gain_masks(rows, cols, spare):
    at = lambda shape, dim: lax.broadcasted_iota(jnp.int32, shape, dim)
    start = at((spare, cols), 0) * rows
    pick = (at((spare, cols), 1) >= start) & (at((spare, cols), 1) < start + rows)
    place = jnp.zeros((rows, cols), jnp.bool_)
    for first in range(0, cols, rows):
        place = place | (at((rows, cols), 1) == at((rows, cols), 0) + first)
    return pick.astype(BF16), place


def project_kernel(me_ref, held_ref, w_ref, res_ref, gain_ref, out_ref, x_ref, *, per_head):
    size, high, width = held_ref.shape
    mine = traced_reversed_bits(me_ref[0], size)
    for t in range(size):
        row = (t % per_head) * high
        col = (t // per_head) * width
        x_ref[row : row + high, col : col + width] = held_ref[mine ^ reversed_bits(t, size)]
    mixed = rows_dot(x_ref[...], w_ref[...])
    rows, cols = res_ref.shape
    out_ref[:, :cols] = (res_ref[...].astype(F32) + mixed).astype(BF16)
    pick, place = gain_masks(rows, cols, out_ref.shape[1] - cols)
    spread = jnp.where(place, gain_ref[...].astype(F32), 0.0).astype(BF16)
    out_ref[:, cols:] = rows_dot(spread, pick).astype(BF16)


def project(me, held, out_proj_t, residual, gain, per_head, spare):
    rows, cols = residual.shape
    return pl.pallas_call(
        functools.partial(project_kernel, per_head=per_head),
        in_specs=[IN_SMEM] + [IN_VMEM] * 4,
        out_specs=IN_VMEM,
        out_shape=pltpu.VMEM((rows, cols + spare), BF16),
        scratch_shapes=[pltpu.VMEM((rows, out_proj_t.shape[1]), BF16)],
        compiler_params=pltpu.CompilerParams(vmem_limit_bytes=MIB + 4 * rows * out_proj_t.shape[1]),
        cost_estimate=HINT,
        name="project",
    )(me, held, out_proj_t, residual, gain)


def feed_kernel(me_ref, held_ref, gate_ref, up_ref, down_hbm, keep_ref, send_ref, x_ref, h_ref, mine_ref, down_ref, sems, *, cols, tile, own):
    size, rows, wide = held_ref.shape
    units, width = down_ref.shape
    chunk = units // sems.shape[0]
    loads = [
        pltpu.make_async_copy(
            down_hbm.at[pl.ds(c * chunk, chunk), :], down_ref.at[pl.ds(c * chunk, chunk), :], sems.at[c]
        )
        for c in range(sems.shape[0])
    ]
    for load in loads:
        load.start()
    me = me_ref[0]
    mine = traced_reversed_bits(me, size)
    squares = jnp.zeros((rows, cols), F32)
    for j in range(size):
        stream = held_ref[j][:, :cols].astype(F32)
        squares = squares + stream * stream
    inverse = lax.rsqrt(jnp.sum(squares, axis=1, keepdims=True) / (cols * size) + 1e-06)
    at = lambda shape, dim: lax.broadcasted_iota(jnp.int32, shape, dim)
    device = me ^ traced_reversed_bits(lax.div(at((rows, rows), 0), own), size)
    order = (at((rows, rows), 1) == device * own + lax.rem(at((rows, rows), 0), own)).astype(BF16)
    pick, place = gain_masks(rows, cols, wide - cols)
    for t in range(size):
        block = held_ref[mine ^ reversed_bits(t, size)]
        spread = jnp.dot(block[:, cols:], pick, preferred_element_type=F32)
        gain = jnp.sum(jnp.where(place, spread, 0.0), axis=0, keepdims=True)
        stream = block[:, :cols]
        part = slice(t * cols, (t + 1) * cols)
        x_ref[:, part] = (stream.astype(F32) * inverse * gain).astype(BF16)
        mine_ref[:, part] = jnp.dot(order[: mine_ref.shape[0]], stream, preferred_element_type=F32)
    for first in range(0, units, tile):
        part = slice(first, min(first + tile, units))
        gate = rows_dot(gate_ref[part, :], x_ref[...])
        up = rows_dot(up_ref[part, :], x_ref[...])
        hidden = (gate * jax.nn.sigmoid(gate) * up).astype(BF16)
        h_ref[:, part] = rows_dot(order, hidden).astype(BF16)
    for load in loads:
        load.wait()
    half = rows // 2
    for first in range(0, width, SPAN):
        part = slice(first, min(first + SPAN, width))
        term = jnp.dot(h_ref[...], down_ref[:, part], preferred_element_type=F32)
        keep_ref[:own, part] = term[:own] + mine_ref[:own, part]
        keep_ref[own:, part] = term[own:half]
        send_ref[:, part] = term[half:].astype(BF16)


def feed(me, held, gate_t, up_t, down_w, cols, own):
    size, rows, wide = held.shape
    units, width = down_w.shape
    tile = 576 if units % 576 == 0 else units
    top = min(rows, -(-own // 16) * 16)
    chunks = 4 if units % 64 == 0 else 1
    kept = 2 * (rows * width + rows * units + units * width) + 4 * top * width
    return pl.pallas_call(
        functools.partial(feed_kernel, cols=cols, tile=tile, own=own),
        in_specs=[IN_SMEM] + [IN_VMEM] * 3 + [pl.BlockSpec(memory_space=pltpu.HBM)],
        out_specs=[IN_VMEM] * 2,
        out_shape=[pltpu.VMEM((rows // 2, width), F32), pltpu.VMEM((rows // 2, width), BF16)],
        scratch_shapes=[
            pltpu.VMEM((rows, width), BF16),
            pltpu.VMEM((rows, units), BF16),
            pltpu.VMEM((top, width), F32),
            pltpu.VMEM((units, width), BF16),
            pltpu.SemaphoreType.DMA((chunks,)),
        ],
        compiler_params=pltpu.CompilerParams(vmem_limit_bytes=2 * MIB + kept + 44 * rows * SPAN),
        name="feed",
    )(me, resident(held), gate_t, up_t, in_hbm(down_w))


def on_device(
    size,
    residual_in,
    queries,
    key_cache,
    value_cache,
    new_keys,
    new_values,
    cache_len,
    tree_mask,
    out_proj,
    norm_gain,
    gate_w,
    up_w,
    down_w,
):
    blocks = queries.shape[0]
    requests = cache_len.shape[0]
    rows, cols = residual_in.shape
    own = rows // size
    me = lax.axis_index("shard").astype(jnp.int32).reshape(1)
    spare = -cols % LANES
    while spare * rows < cols:
        spare += LANES

    attn = attend(
        me, queries, key_cache, value_cache, new_keys, new_values, cache_len, tree_mask
    )
    held = gather(attn, size)
    payload = project(
        me,
        held,
        resident(out_proj.T),
        resident(residual_in),
        resident(norm_gain.reshape(1, cols)),
        requests // blocks,
        spare,
    )
    held = gather(payload, size)
    keep, send = feed(me, held, resident(gate_w.T), resident(up_w.T), down_w, cols, own)
    bit = 1
    while True:
        keep = keep + swap(send, bit, size).astype(F32)
        bit *= 2
        if bit == size:
            return keep.astype(BF16)
        half = keep.shape[0] // 2
        keep, send = keep[:half], keep[half:].astype(BF16)


def solution(mesh):
    placed = (
        P("groups", "shard"),
        P(("groups", "shard"), None, None),
        P(("groups", "shard"), None, None),
        P(("groups", "shard"), None, None),
        P(("groups", "shard"), None, None),
        P(("groups", "shard"), None, None),
        P("groups"),
        P("groups", None, None),
        P(None, "shard"),
        P("shard"),
        P(None, "shard"),
        P(None, "shard"),
        P("shard", None),
    )
    return jax.shard_map(
        functools.partial(on_device, mesh.shape["shard"]),
        mesh=mesh,
        in_specs=placed,
        out_specs=P(("groups", "shard"), None),
        check_vma=False,
    )
```

```python
import functools
import math

import jax
import jax.numpy as jnp
from jax import lax
from jax.experimental import pallas as pl
from jax.experimental.pallas import tpu as pltpu
from jax.sharding import PartitionSpec as P

F32 = jnp.float32
BF16 = jnp.bfloat16
LANES = 128
MIB = 2**20
SPAN = 1024
HINT = pl.CostEstimate(flops=2 * 10**11, bytes_accessed=2 * 10**9, transcendentals=0)
IN_VMEM = pl.BlockSpec(memory_space=pltpu.VMEM)


def resident(x):
    return pltpu.with_memory_space_constraint(x, pltpu.VMEM)


def in_hbm(x):
    return pltpu.with_memory_space_constraint(x, pltpu.HBM)


def rows_dot(a, b):
    return lax.dot_general(a, b, (((1,), (1,)), ((), ())), preferred_element_type=F32)


def reversed_bits(value, size):
    out = value & 0
    low, high = 1, size // 2
    while high:
        out = out + ((value // low) % 2) * high
        low *= 2
        high //= 2
    return out


def traced_reversed_bits(value, size):
    out = value & 0
    low, high = 1, size // 2
    while high:
        out = jnp.where((value & low) != 0, out + high, out)
        low *= 2
        high //= 2
    return out


def swap(x, bit, size):
    return lax.ppermute(x, "shard", [(i, i ^ bit) for i in range(size)])


def join_kernel(first_ref, second_ref, out_ref):
    count = first_ref.shape[0]
    out_ref[:count] = first_ref[...]
    out_ref[count:] = second_ref[...]


def join(first, second):
    count, rows, wide = first.shape
    return pl.pallas_call(
        join_kernel,
        in_specs=[IN_VMEM] * 2,
        out_specs=IN_VMEM,
        out_shape=pltpu.VMEM((2 * count, rows, wide), first.dtype),
        compiler_params=pltpu.CompilerParams(vmem_limit_bytes=MIB),
        name="join",
    )(first, second)


def gather(x, size):
    held = x[None]
    bit = size // 2
    while True:
        other = swap(held, bit, size)
        bit //= 2
        if bit == 0:
            return held, other
        held = join(held, other)


def block_of(near_ref, far_ref, mine, t):
    half = near_ref.shape[0]
    slot = mine ^ reversed_bits(t, 2 * half)
    place = slot & (half - 1)
    return jnp.where(slot < half, near_ref[place], far_ref[place])


def attend_kernel(q_ref, k_ref, v_ref, nk_ref, nv_ref, tree_ref, len_ref, out_ref, score_ref, *, axis, heads, chunk):
    block = pl.program_id(0)
    requests = tree_ref.shape[0]
    request = (lax.axis_index(axis) * pl.num_programs(0) + block) % requests
    length = jnp.sum(
        jnp.where(lax.broadcasted_iota(jnp.int32, (1, requests), 1) == request, len_ref[...], 0),
        axis=1,
        keepdims=True,
    )
    drafts = q_ref.shape[1]
    entries, width = k_ref.shape[1:]
    scale = 1.0 / math.sqrt(width)
    q = jnp.concatenate([q_ref[0][:, g * width : (g + 1) * width] for g in range(heads)], axis=0)
    seen = jnp.concatenate([tree_ref[request]] * heads, axis=0) > 0
    fresh = jnp.where(seen, rows_dot(q, nk_ref[0]) * scale, -1e30)
    position = lax.broadcasted_iota(jnp.int32, (q.shape[0], chunk), 1)
    top = jnp.full((q.shape[0], chunk), -1e30, F32)
    for first in range(0, entries, chunk):
        part = slice(first, first + chunk)
        scores = rows_dot(q, k_ref[0, part, :]) * scale
        scores = jnp.where(position < length - first, scores, -1e30)
        score_ref[:, part] = scores
        top = jnp.maximum(top, scores)
    peak = jnp.maximum(
        jnp.max(top, axis=1, keepdims=True), jnp.max(fresh, axis=1, keepdims=True)
    )
    fresh = jnp.exp(fresh - peak)
    mixed = jnp.dot(fresh.astype(BF16), nv_ref[0], preferred_element_type=F32)
    total = jnp.zeros((q.shape[0], chunk), F32)
    for first in range(0, entries, chunk):
        part = slice(first, first + chunk)
        weights = jnp.exp(score_ref[:, part] - peak)
        total = total + weights
        mixed = mixed + jnp.dot(weights.astype(BF16), v_ref[0, part, :], preferred_element_type=F32)
    denom = jnp.sum(total, axis=1, keepdims=True) + jnp.sum(fresh, axis=1, keepdims=True)
    attn = (mixed / denom).astype(BF16)
    for g in range(heads):
        out_ref[:, g * width : (g + 1) * width] = attn[g * drafts : (g + 1) * drafts]


def attend(axis, queries, key_cache, value_cache, new_keys, new_values, tree_mask, cache_len):
    blocks, drafts, wide = queries.shape
    entries, width = key_cache.shape[1:]
    one = lambda x: pl.BlockSpec((1,) + x.shape[1:], lambda b: (b, 0, 0))
    chunk = 256 if entries % 256 == 0 else entries
    heads = wide // width
    return pl.pallas_call(
        functools.partial(attend_kernel, axis=axis, heads=heads, chunk=chunk),
        grid=(blocks,),
        in_specs=[
            one(queries),
            one(key_cache),
            one(value_cache),
            one(new_keys),
            one(new_values),
            pl.BlockSpec(tree_mask.shape, lambda b: (0, 0, 0)),
            pl.BlockSpec((1, cache_len.shape[0]), lambda b: (0, 0)),
        ],
        out_specs=pl.BlockSpec((drafts, wide), lambda b: (b, 0)),
        out_shape=jax.ShapeDtypeStruct((blocks * drafts, wide), BF16),
        scratch_shapes=[pltpu.VMEM((heads * drafts, entries), F32)],
        compiler_params=pltpu.CompilerParams(
            vmem_limit_bytes=MIB + entries * (8 * width + 4 * heads * drafts)
        ),
        cost_estimate=HINT,
        name="attend",
    )(
        *map(in_hbm, (queries, key_cache, value_cache, new_keys, new_values, tree_mask)),
        in_hbm(cache_len.reshape(1, -1)),
    )


def gain_masks(rows, cols, spare):
    at = lambda shape, dim: lax.broadcasted_iota(jnp.int32, shape, dim)
    start = at((spare, cols), 0) * rows
    pick = (at((spare, cols), 1) >= start) & (at((spare, cols), 1) < start + rows)
    place = jnp.zeros((rows, cols), jnp.bool_)
    for first in range(0, cols, rows):
        place = place | (at((rows, cols), 1) == at((rows, cols), 0) + first)
    return pick.astype(BF16), place


def project_kernel(near_ref, far_ref, w_ref, res_ref, gain_ref, out_ref, x_ref, *, axis, per_head):
    half, high, width = near_ref.shape
    size = 2 * half
    mine = traced_reversed_bits(lax.axis_index(axis), size)
    for t in range(size):
        row = (t % per_head) * high
        col = (t // per_head) * width
        x_ref[row : row + high, col : col + width] = block_of(near_ref, far_ref, mine, t)
    mixed = rows_dot(x_ref[...], w_ref[...])
    rows, cols = res_ref.shape
    out_ref[:, :cols] = (res_ref[...].astype(F32) + mixed).astype(BF16)
    pick, place = gain_masks(rows, cols, out_ref.shape[1] - cols)
    spread = jnp.where(place, gain_ref[...].astype(F32), 0.0).astype(BF16)
    out_ref[:, cols:] = rows_dot(spread, pick).astype(BF16)


def project(axis, near, far, out_proj_t, residual, gain, per_head, spare):
    rows, cols = residual.shape
    return pl.pallas_call(
        functools.partial(project_kernel, axis=axis, per_head=per_head),
        in_specs=[IN_VMEM] * 5,
        out_specs=IN_VMEM,
        out_shape=pltpu.VMEM((rows, cols + spare), BF16),
        scratch_shapes=[pltpu.VMEM((rows, out_proj_t.shape[1]), BF16)],
        compiler_params=pltpu.CompilerParams(vmem_limit_bytes=MIB + 4 * rows * out_proj_t.shape[1]),
        cost_estimate=HINT,
        name="project",
    )(near, far, out_proj_t, residual, gain)


def feed_kernel(near_ref, far_ref, gate_ref, up_ref, down_ref, keep_ref, send_ref, x_ref, h_ref, mine_ref, *, axis, cols, tile, own):
    half, rows, wide = near_ref.shape
    size = 2 * half
    units, width = down_ref.shape
    me = lax.axis_index(axis)
    mine = traced_reversed_bits(me, size)
    squares = jnp.zeros((rows, cols), F32)
    for ref in (near_ref, far_ref):
        for j in range(half):
            stream = ref[j][:, :cols].astype(F32)
            squares = squares + stream * stream
    inverse = lax.rsqrt(jnp.sum(squares, axis=1, keepdims=True) / (cols * size) + 1e-06)
    at = lambda shape, dim: lax.broadcasted_iota(jnp.int32, shape, dim)
    device = me ^ traced_reversed_bits(lax.div(at((rows, rows), 0), own), size)
    order = (at((rows, rows), 1) == device * own + lax.rem(at((rows, rows), 0), own)).astype(BF16)
    pick, place = gain_masks(rows, cols, wide - cols)
    for t in range(size):
        block = block_of(near_ref, far_ref, mine, t)
        spread = jnp.dot(block[:, cols:], pick, preferred_element_type=F32)
        gain = jnp.sum(jnp.where(place, spread, 0.0), axis=0, keepdims=True)
        stream = block[:, :cols]
        part = slice(t * cols, (t + 1) * cols)
        x_ref[:, part] = (stream.astype(F32) * inverse * gain).astype(BF16)
        mine_ref[:, part] = jnp.dot(order[: mine_ref.shape[0]], stream, preferred_element_type=F32)
    for first in range(0, units, tile):
        part = slice(first, min(first + tile, units))
        gate = rows_dot(gate_ref[part, :], x_ref[...])
        up = rows_dot(up_ref[part, :], x_ref[...])
        hidden = (gate * jax.nn.sigmoid(gate) * up).astype(BF16)
        h_ref[:, part] = rows_dot(order, hidden).astype(BF16)
    top = rows // 2
    for first in range(0, width, SPAN):
        part = slice(first, min(first + SPAN, width))
        term = jnp.dot(h_ref[...], down_ref[:, part], preferred_element_type=F32)
        keep_ref[:own, part] = term[:own] + mine_ref[:own, part]
        keep_ref[own:, part] = term[own:top]
        send_ref[:, part] = term[top:].astype(BF16)


def feed(axis, near, far, gate_t, up_t, down_w, cols, own):
    _, rows, wide = near.shape
    units, width = down_w.shape
    tile = 576 if units % 576 == 0 else units
    top = min(rows, -(-own // 16) * 16)
    kept = 2 * (rows * width + rows * units) + 4 * top * width
    return pl.pallas_call(
        functools.partial(feed_kernel, axis=axis, cols=cols, tile=tile, own=own),
        in_specs=[IN_VMEM] * 5,
        out_specs=[IN_VMEM] * 2,
        out_shape=[pltpu.VMEM((rows // 2, width), F32), pltpu.VMEM((rows // 2, width), BF16)],
        scratch_shapes=[
            pltpu.VMEM((rows, width), BF16),
            pltpu.VMEM((rows, units), BF16),
            pltpu.VMEM((top, width), F32),
        ],
        compiler_params=pltpu.CompilerParams(vmem_limit_bytes=8 * MIB + kept + 44 * (rows - min(rows, 64)) * SPAN),
        name="feed",
    )(resident(near), resident(far), gate_t, up_t, resident(down_w))


def on_device(
    size,
    residual_in,
    queries,
    key_cache,
    value_cache,
    new_keys,
    new_values,
    cache_len,
    tree_mask,
    out_proj,
    norm_gain,
    gate_w,
    up_w,
    down_w,
):
    blocks = queries.shape[0]
    requests = cache_len.shape[0]
    rows, cols = residual_in.shape
    own = rows // size
    spare = -cols % LANES
    while spare * rows < cols:
        spare += LANES

    gain, queries = lax.optimization_barrier((norm_gain.reshape(1, cols), queries))
    attn = attend(
        "shard", queries, key_cache, value_cache, new_keys, new_values, tree_mask, cache_len
    )
    near, far = gather(attn, size)
    payload = project(
        "shard",
        near,
        far,
        resident(out_proj.T),
        resident(residual_in),
        resident(gain),
        requests // blocks,
        spare,
    )
    near, far = gather(payload, size)
    keep, send = feed("shard", near, far, resident(gate_w.T), resident(up_w.T), down_w, cols, own)
    bit = 1
    while True:
        keep = keep + swap(send, bit, size).astype(F32)
        bit *= 2
        if bit == size:
            return keep.astype(BF16)
        half = keep.shape[0] // 2
        keep, send = keep[:half], keep[half:].astype(BF16)


def solution(mesh):
    placed = (
        P("groups", "shard"),
        P(("groups", "shard"), None, None),
        P(("groups", "shard"), None, None),
        P(("groups", "shard"), None, None),
        P(("groups", "shard"), None, None),
        P(("groups", "shard"), None, None),
        P("groups"),
        P("groups", None, None),
        P(None, "shard"),
        P("shard"),
        P(None, "shard"),
        P(None, "shard"),
        P("shard", None),
    )
    return jax.shard_map(
        functools.partial(on_device, mesh.shape["shard"]),
        mesh=mesh,
        in_specs=placed,
        out_specs=P(("groups", "shard"), None),
        check_vma=False,
    )
```

```python
import functools
import math

import jax
import jax.numpy as jnp
from jax import lax
from jax.experimental import pallas as pl
from jax.experimental.pallas import tpu as pltpu
from jax.sharding import PartitionSpec as P

F32 = jnp.float32
BF16 = jnp.bfloat16
LANES = 128
MIB = 2**20
SPAN = 1024
HINT = pl.CostEstimate(flops=2 * 10**11, bytes_accessed=2 * 10**9, transcendentals=0)
IN_VMEM = pl.BlockSpec(memory_space=pltpu.VMEM)


def resident(x):
    return pltpu.with_memory_space_constraint(x, pltpu.VMEM)


def in_hbm(x):
    return pltpu.with_memory_space_constraint(x, pltpu.HBM)


def rows_dot(a, b):
    return lax.dot_general(a, b, (((1,), (1,)), ((), ())), preferred_element_type=F32)


def reversed_bits(value, size):
    out = value & 0
    low, high = 1, size // 2
    while high:
        out = out + ((value // low) % 2) * high
        low *= 2
        high //= 2
    return out


def traced_reversed_bits(value, size):
    out = value & 0
    low, high = 1, size // 2
    while high:
        out = jnp.where((value & low) != 0, out + high, out)
        low *= 2
        high //= 2
    return out


def swap(x, bit, size):
    return lax.ppermute(x, "shard", [(i, i ^ bit) for i in range(size)])


def join_kernel(*refs):
    *pieces, out_ref = refs
    first = 0
    for piece in pieces:
        out_ref[first : first + piece.shape[0]] = piece[...]
        first += piece.shape[0]


def join(*pieces):
    count = sum(piece.shape[0] for piece in pieces)
    return pl.pallas_call(
        join_kernel,
        in_specs=[IN_VMEM] * len(pieces),
        out_specs=IN_VMEM,
        out_shape=pltpu.VMEM((count,) + pieces[0].shape[1:], pieces[0].dtype),
        compiler_params=pltpu.CompilerParams(vmem_limit_bytes=MIB),
        name="join",
    )(*pieces)


def gather(x, size):
    held = x[None]
    bit = size // 2
    if size > 4:
        low = bit // 2
        held = join(held, *(swap(held, way, size) for way in (bit, low, bit + low)))
        bit = low // 2
    while True:
        other = swap(held, bit, size)
        bit //= 2
        if bit == 0:
            return held, other
        held = join(held, other)


def block_of(near_ref, far_ref, mine, t):
    half = near_ref.shape[0]
    slot = mine ^ reversed_bits(t, 2 * half)
    place = slot & (half - 1)
    return jnp.where(slot < half, near_ref[place], far_ref[place])


def attend_kernel(q_ref, k_ref, v_ref, nk_ref, nv_ref, tree_ref, len_ref, out_ref, score_ref, *, axis, heads, chunk):
    block = pl.program_id(0)
    requests = tree_ref.shape[0]
    request = (lax.axis_index(axis) * pl.num_programs(0) + block) % requests
    length = jnp.sum(
        jnp.where(lax.broadcasted_iota(jnp.int32, (1, requests), 1) == request, len_ref[...], 0),
        axis=1,
        keepdims=True,
    )
    drafts = q_ref.shape[1]
    entries, width = k_ref.shape[1:]
    scale = 1.0 / math.sqrt(width)
    q = jnp.concatenate([q_ref[0][:, g * width : (g + 1) * width] for g in range(heads)], axis=0)
    seen = jnp.concatenate([tree_ref[request]] * heads, axis=0) > 0
    fresh = jnp.where(seen, rows_dot(q, nk_ref[0]) * scale, -1e30)
    position = lax.broadcasted_iota(jnp.int32, (q.shape[0], chunk), 1)
    top = jnp.full((q.shape[0], chunk), -1e30, F32)
    for first in range(0, entries, chunk):
        part = slice(first, first + chunk)
        scores = rows_dot(q, k_ref[0, part, :]) * scale
        scores = jnp.where(position < length - first, scores, -1e30)
        score_ref[:, part] = scores
        top = jnp.maximum(top, scores)
    peak = jnp.maximum(
        jnp.max(top, axis=1, keepdims=True), jnp.max(fresh, axis=1, keepdims=True)
    )
    fresh = jnp.exp(fresh - peak)
    mixed = jnp.dot(fresh.astype(BF16), nv_ref[0], preferred_element_type=F32)
    total = jnp.zeros((q.shape[0], chunk), F32)
    for first in range(0, entries, chunk):
        part = slice(first, first + chunk)
        weights = jnp.exp(score_ref[:, part] - peak)
        total = total + weights
        mixed = mixed + jnp.dot(weights.astype(BF16), v_ref[0, part, :], preferred_element_type=F32)
    denom = jnp.sum(total, axis=1, keepdims=True) + jnp.sum(fresh, axis=1, keepdims=True)
    attn = (mixed / denom).astype(BF16)
    for g in range(heads):
        out_ref[:, g * width : (g + 1) * width] = attn[g * drafts : (g + 1) * drafts]


def attend(axis, queries, key_cache, value_cache, new_keys, new_values, tree_mask, cache_len):
    blocks, drafts, wide = queries.shape
    entries, width = key_cache.shape[1:]
    one = lambda x: pl.BlockSpec((1,) + x.shape[1:], lambda b: (b, 0, 0))
    chunk = 256 if entries % 256 == 0 else entries
    heads = wide // width
    return pl.pallas_call(
        functools.partial(attend_kernel, axis=axis, heads=heads, chunk=chunk),
        grid=(blocks,),
        in_specs=[
            one(queries),
            one(key_cache),
            one(value_cache),
            one(new_keys),
            one(new_values),
            pl.BlockSpec(tree_mask.shape, lambda b: (0, 0, 0)),
            pl.BlockSpec((1, cache_len.shape[0]), lambda b: (0, 0)),
        ],
        out_specs=pl.BlockSpec((drafts, wide), lambda b: (b, 0)),
        out_shape=jax.ShapeDtypeStruct((blocks * drafts, wide), BF16),
        scratch_shapes=[pltpu.VMEM((heads * drafts, entries), F32)],
        compiler_params=pltpu.CompilerParams(
            vmem_limit_bytes=MIB + entries * (8 * width + 4 * heads * drafts)
        ),
        cost_estimate=HINT,
        name="attend",
    )(
        *map(in_hbm, (queries, key_cache, value_cache, new_keys, new_values, tree_mask)),
        in_hbm(cache_len.reshape(1, -1)),
    )


def packing(rows, cols):
    full, rest = divmod(cols, LANES)
    fold = LANES // rest if rest and LANES % rest == 0 and rows % (16 * (LANES // rest)) == 0 else 1
    high = rows // fold if rest else 0
    gain_at = full * rows + high
    return full, rest, fold, high, gain_at, gain_at + -(-(full + (rest > 0)) // 8) * 8


def project_kernel(near_ref, far_ref, w_ref, res_ref, gain_ref, out_ref, x_ref, *, axis, per_head):
    half, high, width = near_ref.shape
    size = 2 * half
    mine = traced_reversed_bits(lax.axis_index(axis), size)
    for t in range(size):
        row = (t % per_head) * high
        col = (t // per_head) * width
        x_ref[row : row + high, col : col + width] = block_of(near_ref, far_ref, mine, t)
    mixed = rows_dot(x_ref[...], w_ref[...])
    rows, cols = res_ref.shape
    stream = (res_ref[...].astype(F32) + mixed).astype(BF16)
    full, rest, fold, high, gain_at, total = packing(rows, cols)
    for i in range(full):
        out_ref[i * rows : (i + 1) * rows, :] = stream[:, i * LANES : (i + 1) * LANES]
    if rest:
        narrow = stream[:, full * LANES :]
        parts = [narrow[q * high : (q + 1) * high] for q in range(fold)]
        if fold * rest < LANES:
            parts.append(jnp.zeros((high, LANES - fold * rest), BF16))
        out_ref[full * rows : gain_at, :] = jnp.concatenate(parts, axis=1)
    gain = jnp.concatenate(
        [gain_ref[...].astype(F32), jnp.zeros((1, (total - gain_at) * LANES - cols), F32)], axis=1
    )
    out_ref[gain_at:, :] = jnp.concatenate(
        [gain[:, i * LANES : (i + 1) * LANES] for i in range(total - gain_at)], axis=0
    ).astype(BF16)


def project(axis, near, far, out_proj_t, residual, gain, per_head):
    rows, cols = residual.shape
    return pl.pallas_call(
        functools.partial(project_kernel, axis=axis, per_head=per_head),
        in_specs=[IN_VMEM] * 5,
        out_specs=IN_VMEM,
        out_shape=pltpu.VMEM((packing(rows, cols)[-1], LANES), BF16),
        scratch_shapes=[pltpu.VMEM((rows, out_proj_t.shape[1]), BF16)],
        compiler_params=pltpu.CompilerParams(vmem_limit_bytes=MIB + 4 * rows * out_proj_t.shape[1]),
        cost_estimate=HINT,
        name="project",
    )(near, far, out_proj_t, residual, gain)


def feed_kernel(near_ref, far_ref, gate_ref, up_ref, down_ref, keep_ref, send_ref, x_ref, h_ref, mine_ref, gain_ref, *, axis, rows, tile, own):
    size = 2 * near_ref.shape[0]
    units, width = down_ref.shape
    cols = width // size
    full, rest, fold, high, gain_at, _ = packing(rows, cols)
    me = lax.axis_index(axis)
    mine = traced_reversed_bits(me, size)
    squares = jnp.zeros((rows, cols), F32)
    for t in range(size):
        block = block_of(near_ref, far_ref, mine, t)
        pieces = [block[i * rows : (i + 1) * rows] for i in range(full)]
        gains = [block[gain_at + i : gain_at + i + 1].astype(F32) for i in range(full)]
        if rest:
            narrow = block[full * rows : gain_at]
            pieces.append(
                jnp.concatenate([narrow[:, q * rest : (q + 1) * rest] for q in range(fold)], axis=0)
            )
            gains.append(block[gain_at + full : gain_at + full + 1, :rest].astype(F32))
        stream = jnp.concatenate(pieces, axis=1)
        part = slice(t * cols, (t + 1) * cols)
        x_ref[:, part] = stream
        gain_ref[:, part] = jnp.concatenate(gains, axis=1)
        wide = stream.astype(F32)
        squares = squares + wide * wide
    inverse = lax.rsqrt(jnp.sum(squares, axis=1, keepdims=True) / width + 1e-06)
    at = lambda shape, dim: lax.broadcasted_iota(jnp.int32, shape, dim)
    device = me ^ traced_reversed_bits(lax.div(at((rows, rows), 0), own), size)
    order = (at((rows, rows), 1) == device * own + lax.rem(at((rows, rows), 0), own)).astype(BF16)
    for first in range(0, width, SPAN):
        part = slice(first, min(first + SPAN, width))
        stream = x_ref[:, part]
        mine_ref[:, part] = jnp.dot(order[: mine_ref.shape[0]], stream, preferred_element_type=F32)
        x_ref[:, part] = (stream.astype(F32) * inverse * gain_ref[:, part]).astype(BF16)
    for first in range(0, units, tile):
        part = slice(first, min(first + tile, units))
        gate = rows_dot(gate_ref[part, :], x_ref[...])
        up = rows_dot(up_ref[part, :], x_ref[...])
        hidden = (gate * jax.nn.sigmoid(gate) * up).astype(BF16)
        h_ref[:, part] = rows_dot(order, hidden).astype(BF16)
    top = rows // 2
    for first in range(0, width, SPAN):
        part = slice(first, min(first + SPAN, width))
        term = jnp.dot(h_ref[...], down_ref[:, part], preferred_element_type=F32)
        keep_ref[:own, part] = term[:own] + mine_ref[:own, part]
        keep_ref[own:, part] = term[own:top]
        send_ref[:, part] = term[top:].astype(BF16)


def feed(axis, near, far, gate_t, up_t, down_w, rows, own):
    units, width = down_w.shape
    tile = 576 if units % 576 == 0 else units
    top = min(rows, -(-own // 16) * 16)
    kept = 2 * (rows * width + rows * units) + 4 * top * width
    return pl.pallas_call(
        functools.partial(feed_kernel, axis=axis, rows=rows, tile=tile, own=own),
        in_specs=[IN_VMEM] * 5,
        out_specs=[IN_VMEM] * 2,
        out_shape=[pltpu.VMEM((rows // 2, width), F32), pltpu.VMEM((rows // 2, width), BF16)],
        scratch_shapes=[
            pltpu.VMEM((rows, width), BF16),
            pltpu.VMEM((rows, units), BF16),
            pltpu.VMEM((top, width), F32),
            pltpu.VMEM((1, width), F32),
        ],
        compiler_params=pltpu.CompilerParams(vmem_limit_bytes=8 * MIB + kept + 44 * (rows - min(rows, 64)) * SPAN),
        name="feed",
    )(resident(near), resident(far), gate_t, up_t, resident(down_w))


def on_device(
    size,
    residual_in,
    queries,
    key_cache,
    value_cache,
    new_keys,
    new_values,
    cache_len,
    tree_mask,
    out_proj,
    norm_gain,
    gate_w,
    up_w,
    down_w,
):
    blocks = queries.shape[0]
    requests = cache_len.shape[0]
    rows, cols = residual_in.shape
    own = rows // size
    gain, queries = lax.optimization_barrier((norm_gain.reshape(1, cols), queries))
    attn = attend(
        "shard", queries, key_cache, value_cache, new_keys, new_values, tree_mask, cache_len
    )
    near, far = gather(attn, size)
    payload = project(
        "shard",
        near,
        far,
        resident(out_proj.T),
        resident(residual_in),
        resident(gain),
        requests // blocks,
    )
    near, far = gather(payload, size)
    keep, send = feed("shard", near, far, resident(gate_w.T), resident(up_w.T), down_w, rows, own)
    bit = 1
    while True:
        keep = keep + swap(send, bit, size).astype(F32)
        bit *= 2
        if bit == size:
            return keep.astype(BF16)
        half = keep.shape[0] // 2
        keep, send = keep[:half], keep[half:].astype(BF16)


def solution(mesh):
    placed = (
        P("groups", "shard"),
        P(("groups", "shard"), None, None),
        P(("groups", "shard"), None, None),
        P(("groups", "shard"), None, None),
        P(("groups", "shard"), None, None),
        P(("groups", "shard"), None, None),
        P("groups"),
        P("groups", None, None),
        P(None, "shard"),
        P("shard"),
        P(None, "shard"),
        P(None, "shard"),
        P("shard", None),
    )
    return jax.shard_map(
        functools.partial(on_device, mesh.shape["shard"]),
        mesh=mesh,
        in_specs=placed,
        out_specs=P(("groups", "shard"), None),
        check_vma=False,
    )
```

```python
import functools
import math

import jax
import jax.numpy as jnp
from jax import lax
from jax.experimental import pallas as pl
from jax.experimental.pallas import tpu as pltpu
from jax.sharding import PartitionSpec as P

F32 = jnp.float32
BF16 = jnp.bfloat16
LANES = 128
MIB = 2**20
SPAN = 1024
HINT = pl.CostEstimate(flops=2 * 10**11, bytes_accessed=2 * 10**9, transcendentals=0)
IN_VMEM = pl.BlockSpec(memory_space=pltpu.VMEM)


def resident(x):
    return pltpu.with_memory_space_constraint(x, pltpu.VMEM)


def in_hbm(x):
    return pltpu.with_memory_space_constraint(x, pltpu.HBM)


def rows_dot(a, b):
    return lax.dot_general(a, b, (((1,), (1,)), ((), ())), preferred_element_type=F32)


def reversed_bits(value, size):
    out = value & 0
    low, high = 1, size // 2
    while high:
        out = out + ((value // low) % 2) * high
        low *= 2
        high //= 2
    return out


def traced_reversed_bits(value, size):
    out = value & 0
    low, high = 1, size // 2
    while high:
        out = jnp.where((value & low) != 0, out + high, out)
        low *= 2
        high //= 2
    return out


def swap(x, bit, size):
    return lax.ppermute(x, "shard", [(i, i ^ bit) for i in range(size)])


def join_kernel(*refs):
    *pieces, out_ref = refs
    first = 0
    for piece in pieces:
        out_ref[first : first + piece.shape[0]] = piece[...]
        first += piece.shape[0]


def join(*pieces):
    count = sum(piece.shape[0] for piece in pieces)
    return pl.pallas_call(
        join_kernel,
        in_specs=[IN_VMEM] * len(pieces),
        out_specs=IN_VMEM,
        out_shape=pltpu.VMEM((count,) + pieces[0].shape[1:], pieces[0].dtype),
        compiler_params=pltpu.CompilerParams(vmem_limit_bytes=MIB),
        name="join",
    )(*pieces)


def gather(x, size):
    held = x[None]
    bit = size // 2
    if size > 4:
        low = bit // 2
        near, far, both = (swap(held, way, size) for way in (low, bit, bit + low))
        held = join(held, far, near, both)
        bit = low // 2
    while True:
        other = swap(held, bit, size)
        bit //= 2
        if bit == 0:
            return held, other
        held = join(held, other)


def block_of(near_ref, far_ref, mine, t):
    half = near_ref.shape[0]
    slot = mine ^ reversed_bits(t, 2 * half)
    place = slot & (half - 1)
    return jnp.where(slot < half, near_ref[place], far_ref[place])


def attend_kernel(q_ref, nk_ref, nv_ref, tree_ref, len_ref, k_hbm, v_hbm, out_ref, k_ref, v_ref, score_ref, sems, *, axis, heads, chunk):
    blocks, drafts = q_ref.shape[:2]
    loads = [
        [
            pltpu.make_async_copy(hbm.at[b], ref.at[b], sems.at[which, b])
            for which, (hbm, ref) in enumerate(((k_hbm, k_ref), (v_hbm, v_ref)))
        ]
        for b in range(blocks)
    ]
    for pair in loads:
        for load in pair:
            load.start()
    requests = tree_ref.shape[0]
    entries, width = k_ref.shape[1:]
    scale = 1.0 / math.sqrt(width)
    for b in range(blocks):
        request = (lax.axis_index(axis) * blocks + b) % requests
        length = jnp.sum(
            jnp.where(lax.broadcasted_iota(jnp.int32, (1, requests), 1) == request, len_ref[...], 0),
            axis=1,
            keepdims=True,
        )
        q = jnp.concatenate([q_ref[b][:, g * width : (g + 1) * width] for g in range(heads)], axis=0)
        seen = jnp.concatenate([tree_ref[request]] * heads, axis=0) > 0
        fresh = jnp.where(seen, rows_dot(q, nk_ref[b]) * scale, -1e30)
        position = lax.broadcasted_iota(jnp.int32, (q.shape[0], chunk), 1)
        top = jnp.full((q.shape[0], chunk), -1e30, F32)
        loads[b][0].wait()
        for first in range(0, entries, chunk):
            part = slice(first, first + chunk)
            scores = rows_dot(q, k_ref[b, part, :]) * scale
            scores = jnp.where(position < length - first, scores, -1e30)
            score_ref[:, part] = scores
            top = jnp.maximum(top, scores)
        peak = jnp.maximum(
            jnp.max(top, axis=1, keepdims=True), jnp.max(fresh, axis=1, keepdims=True)
        )
        fresh = jnp.exp(fresh - peak)
        mixed = jnp.dot(fresh.astype(BF16), nv_ref[b], preferred_element_type=F32)
        total = jnp.zeros((q.shape[0], chunk), F32)
        loads[b][1].wait()
        for first in range(0, entries, chunk):
            part = slice(first, first + chunk)
            weights = jnp.exp(score_ref[:, part] - peak)
            total = total + weights
            mixed = mixed + jnp.dot(
                weights.astype(BF16), v_ref[b, part, :], preferred_element_type=F32
            )
        denom = jnp.sum(total, axis=1, keepdims=True) + jnp.sum(fresh, axis=1, keepdims=True)
        attn = (mixed / denom).astype(BF16)
        for g in range(heads):
            out_ref[b * drafts : (b + 1) * drafts, g * width : (g + 1) * width] = attn[
                g * drafts : (g + 1) * drafts
            ]


def attend(axis, queries, key_cache, value_cache, new_keys, new_values, tree_mask, cache_len):
    blocks, drafts, wide = queries.shape
    entries, width = key_cache.shape[1:]
    chunk = 256 if entries % 256 == 0 else entries
    heads = wide // width
    return pl.pallas_call(
        functools.partial(attend_kernel, axis=axis, heads=heads, chunk=chunk),
        in_specs=[IN_VMEM] * 5 + [pl.BlockSpec(memory_space=pltpu.HBM)] * 2,
        out_specs=IN_VMEM,
        out_shape=pltpu.VMEM((blocks * drafts, wide), BF16),
        scratch_shapes=[
            pltpu.VMEM(key_cache.shape, BF16),
            pltpu.VMEM(value_cache.shape, BF16),
            pltpu.VMEM((heads * drafts, entries), F32),
            pltpu.SemaphoreType.DMA((2, blocks)),
        ],
        compiler_params=pltpu.CompilerParams(
            vmem_limit_bytes=MIB + entries * 4 * (blocks * width + heads * drafts)
        ),
        cost_estimate=HINT,
        name="attend",
    )(
        *map(in_hbm, (queries, new_keys, new_values, tree_mask, cache_len.reshape(1, -1))),
        in_hbm(key_cache),
        in_hbm(value_cache),
    )


def packing(rows, cols):
    full, rest = divmod(cols, LANES)
    fold = LANES // rest if rest and LANES % rest == 0 and rows % (16 * (LANES // rest)) == 0 else 1
    high = rows // fold if rest else 0
    gain_at = full * rows + high
    return full, rest, fold, high, gain_at, gain_at + -(-(full + (rest > 0)) // 8) * 8


def project_kernel(near_ref, far_ref, w_ref, res_ref, gain_ref, out_ref, x_ref, *, axis, per_head):
    half, high, width = near_ref.shape
    size = 2 * half
    mine = traced_reversed_bits(lax.axis_index(axis), size)
    for t in range(size):
        row = (t % per_head) * high
        col = (t // per_head) * width
        x_ref[row : row + high, col : col + width] = block_of(near_ref, far_ref, mine, t)
    mixed = rows_dot(x_ref[...], w_ref[...])
    rows, cols = res_ref.shape
    stream = (res_ref[...].astype(F32) + mixed).astype(BF16)
    full, rest, fold, high, gain_at, total = packing(rows, cols)
    for i in range(full):
        out_ref[i * rows : (i + 1) * rows, :] = stream[:, i * LANES : (i + 1) * LANES]
    if rest:
        narrow = stream[:, full * LANES :]
        parts = [narrow[q * high : (q + 1) * high] for q in range(fold)]
        if fold * rest < LANES:
            parts.append(jnp.zeros((high, LANES - fold * rest), BF16))
        out_ref[full * rows : gain_at, :] = jnp.concatenate(parts, axis=1)
    gain = jnp.concatenate(
        [gain_ref[...].astype(F32).reshape(1, cols), jnp.zeros((1, (total - gain_at) * LANES - cols), F32)], axis=1
    )
    out_ref[gain_at:, :] = jnp.concatenate(
        [gain[:, i * LANES : (i + 1) * LANES] for i in range(total - gain_at)], axis=0
    ).astype(BF16)


def project(axis, near, far, out_proj_t, residual, gain, per_head):
    rows, cols = residual.shape
    return pl.pallas_call(
        functools.partial(project_kernel, axis=axis, per_head=per_head),
        in_specs=[IN_VMEM] * 5,
        out_specs=IN_VMEM,
        out_shape=pltpu.VMEM((packing(rows, cols)[-1], LANES), BF16),
        scratch_shapes=[pltpu.VMEM((rows, out_proj_t.shape[1]), BF16)],
        compiler_params=pltpu.CompilerParams(vmem_limit_bytes=MIB + 4 * rows * out_proj_t.shape[1]),
        cost_estimate=HINT,
        name="project",
    )(near, far, out_proj_t, residual, gain)


def feed_kernel(near_ref, far_ref, gate_ref, up_ref, down_ref, keep_ref, send_ref, x_ref, h_ref, mine_ref, gain_ref, *, axis, rows, tile, own):
    size = 2 * near_ref.shape[0]
    units, width = down_ref.shape
    cols = width // size
    full, rest, fold, high, gain_at, _ = packing(rows, cols)
    me = lax.axis_index(axis)
    mine = traced_reversed_bits(me, size)
    squares = jnp.zeros((rows, cols), F32)
    for t in range(size):
        block = block_of(near_ref, far_ref, mine, t)
        pieces = [block[i * rows : (i + 1) * rows] for i in range(full)]
        gains = [block[gain_at + i : gain_at + i + 1].astype(F32) for i in range(full)]
        if rest:
            narrow = block[full * rows : gain_at]
            pieces.append(
                jnp.concatenate([narrow[:, q * rest : (q + 1) * rest] for q in range(fold)], axis=0)
            )
            gains.append(block[gain_at + full : gain_at + full + 1, :rest].astype(F32))
        stream = jnp.concatenate(pieces, axis=1)
        part = slice(t * cols, (t + 1) * cols)
        x_ref[:, part] = stream
        gain_ref[:, part] = jnp.concatenate(gains, axis=1)
        wide = stream.astype(F32)
        squares = squares + wide * wide
    inverse = lax.rsqrt(jnp.sum(squares, axis=1, keepdims=True) / width + 1e-06)
    at = lambda shape, dim: lax.broadcasted_iota(jnp.int32, shape, dim)
    device = me ^ traced_reversed_bits(lax.div(at((rows, rows), 0), own), size)
    order = (at((rows, rows), 1) == device * own + lax.rem(at((rows, rows), 0), own)).astype(BF16)
    for first in range(0, width, SPAN):
        part = slice(first, min(first + SPAN, width))
        stream = x_ref[:, part]
        mine_ref[:, part] = jnp.dot(order[: mine_ref.shape[0]], stream, preferred_element_type=F32)
        x_ref[:, part] = (stream.astype(F32) * inverse * gain_ref[:, part]).astype(BF16)
    for first in range(0, units, tile):
        part = slice(first, min(first + tile, units))
        gate = rows_dot(gate_ref[part, :], x_ref[...])
        up = rows_dot(up_ref[part, :], x_ref[...])
        hidden = (gate * jax.nn.sigmoid(gate) * up).astype(BF16)
        h_ref[:, part] = rows_dot(order, hidden).astype(BF16)
    top = rows // 2
    for first in range(0, width, SPAN):
        part = slice(first, min(first + SPAN, width))
        term = jnp.dot(h_ref[...], down_ref[:, part], preferred_element_type=F32)
        keep_ref[:own, part] = term[:own] + mine_ref[:own, part]
        keep_ref[own:, part] = term[own:top]
        send_ref[:, part] = term[top:].astype(BF16)


def feed(axis, near, far, gate_t, up_t, down_w, rows, own):
    units, width = down_w.shape
    tile = 576 if units % 576 == 0 else units
    top = min(rows, -(-own // 16) * 16)
    kept = 2 * (rows * width + rows * units) + 4 * top * width
    return pl.pallas_call(
        functools.partial(feed_kernel, axis=axis, rows=rows, tile=tile, own=own),
        in_specs=[IN_VMEM] * 5,
        out_specs=[IN_VMEM] * 2,
        out_shape=[pltpu.VMEM((rows // 2, width), F32), pltpu.VMEM((rows // 2, width), BF16)],
        scratch_shapes=[
            pltpu.VMEM((rows, width), BF16),
            pltpu.VMEM((rows, units), BF16),
            pltpu.VMEM((top, width), F32),
            pltpu.VMEM((1, width), F32),
        ],
        compiler_params=pltpu.CompilerParams(vmem_limit_bytes=8 * MIB + kept + 44 * (rows - min(rows, 64)) * SPAN),
        name="feed",
    )(resident(near), resident(far), gate_t, up_t, resident(down_w))


def on_device(
    size,
    residual_in,
    queries,
    key_cache,
    value_cache,
    new_keys,
    new_values,
    cache_len,
    tree_mask,
    out_proj,
    norm_gain,
    gate_w,
    up_w,
    down_w,
):
    blocks = queries.shape[0]
    requests = cache_len.shape[0]
    rows, cols = residual_in.shape
    own = rows // size
    gain = norm_gain
    attn = attend(
        "shard", queries, key_cache, value_cache, new_keys, new_values, tree_mask, cache_len
    )
    near, far = gather(attn, size)
    payload = project(
        "shard",
        near,
        far,
        resident(out_proj.T),
        resident(residual_in),
        resident(gain),
        requests // blocks,
    )
    near, far = gather(payload, size)
    keep, send = feed("shard", near, far, resident(gate_w.T), resident(up_w.T), down_w, rows, own)
    bit = 1
    while 4 * own < keep.shape[0] or size <= 4:
        keep = keep + swap(send, bit, size).astype(F32)
        bit *= 2
        if bit == size:
            return keep.astype(BF16)
        half = keep.shape[0] // 2
        keep, send = keep[:half], keep[half:].astype(BF16)
    keep = keep + swap(send, bit, size).astype(F32)
    low, high = size // 4, size // 2
    both = swap(keep[3 * own :].astype(BF16), low + high, size)
    far = swap(keep[own : 2 * own].astype(BF16), high, size)
    near = swap(keep[2 * own : 3 * own].astype(BF16), low, size)
    return (keep[:own] + both.astype(F32) + far.astype(F32) + near.astype(F32)).astype(BF16)


def solution(mesh):
    placed = (
        P("groups", "shard"),
        P(("groups", "shard"), None, None),
        P(("groups", "shard"), None, None),
        P(("groups", "shard"), None, None),
        P(("groups", "shard"), None, None),
        P(("groups", "shard"), None, None),
        P("groups"),
        P("groups", None, None),
        P(None, "shard"),
        P("shard"),
        P(None, "shard"),
        P(None, "shard"),
        P("shard", None),
    )
    return jax.shard_map(
        functools.partial(on_device, mesh.shape["shard"]),
        mesh=mesh,
        in_specs=placed,
        out_specs=P(("groups", "shard"), None),
        check_vma=False,
    )
```

```python
import functools
import math

import jax
import jax.numpy as jnp
from jax import lax
from jax.experimental import pallas as pl
from jax.experimental.pallas import tpu as pltpu
from jax.sharding import PartitionSpec as P

F32 = jnp.float32
BF16 = jnp.bfloat16
LANES = 128
MIB = 2**20
SPAN = 1024
HINT = pl.CostEstimate(flops=2 * 10**11, bytes_accessed=2 * 10**9, transcendentals=0)
IN_VMEM = pl.BlockSpec(memory_space=pltpu.VMEM)


def resident(x):
    return pltpu.with_memory_space_constraint(x, pltpu.VMEM)


def in_hbm(x):
    return pltpu.with_memory_space_constraint(x, pltpu.HBM)


def rows_dot(a, b):
    return lax.dot_general(a, b, (((1,), (1,)), ((), ())), preferred_element_type=F32)


def reversed_bits(value, size):
    out = value & 0
    low, high = 1, size // 2
    while high:
        out = out + ((value // low) % 2) * high
        low *= 2
        high //= 2
    return out


def traced_reversed_bits(value, size):
    out = value & 0
    low, high = 1, size // 2
    while high:
        out = jnp.where((value & low) != 0, out + high, out)
        low *= 2
        high //= 2
    return out


def swap(x, bit, size):
    return lax.ppermute(x, "shard", [(i, i ^ bit) for i in range(size)])


def join_kernel(*refs):
    *pieces, out_ref = refs
    first = 0
    for piece in pieces:
        out_ref[first : first + piece.shape[0]] = piece[...]
        first += piece.shape[0]


def join(*pieces, hint=None):
    count = sum(piece.shape[0] for piece in pieces)
    return pl.pallas_call(
        join_kernel,
        in_specs=[IN_VMEM] * len(pieces),
        out_specs=IN_VMEM,
        out_shape=pltpu.VMEM((count,) + pieces[0].shape[1:], pieces[0].dtype),
        compiler_params=pltpu.CompilerParams(vmem_limit_bytes=MIB),
        cost_estimate=hint,
        name="join",
    )(*pieces)


def gather(x, size, hint=None):
    held = x[None]
    bit = size // 2
    if size > 4:
        low = bit // 2
        near, far, both = (swap(held, way, size) for way in (low, bit, bit + low))
        held = join(held, far, near, both, hint=hint)
        bit = low // 2
    while True:
        other = swap(held, bit, size)
        bit //= 2
        if bit == 0:
            return held, other
        held = join(held, other)


def block_of(near_ref, far_ref, mine, t):
    half = near_ref.shape[0]
    slot = mine ^ reversed_bits(t, 2 * half)
    place = slot & (half - 1)
    return jnp.where(slot < half, near_ref[place], far_ref[place])


def attend_kernel(*refs, axis, heads, chunk):
    *sources, k_hbm, v_hbm, out_ref, q_ref, nk_ref, nv_ref, tree_ref, len_ref, k_ref, v_ref, score_ref, small_sems, sems = refs
    blocks, drafts = q_ref.shape[:2]
    small = [
        pltpu.make_async_copy(source, ref, small_sems.at[i])
        for i, (source, ref) in enumerate(zip(sources, (q_ref, nk_ref, nv_ref, tree_ref, len_ref)))
    ]
    for load in small:
        load.start()
    loads = [
        [
            pltpu.make_async_copy(hbm.at[b], ref.at[b], sems.at[which, b])
            for which, (hbm, ref) in enumerate(((k_hbm, k_ref), (v_hbm, v_ref)))
        ]
        for b in range(blocks)
    ]
    for pair in loads:
        for load in pair:
            load.start()
    for load in small:
        load.wait()
    requests = tree_ref.shape[0]
    entries, width = k_ref.shape[1:]
    scale = 1.0 / math.sqrt(width)
    for b in range(blocks):
        request = (lax.axis_index(axis) * blocks + b) % requests
        length = jnp.sum(
            jnp.where(lax.broadcasted_iota(jnp.int32, (1, requests), 1) == request, len_ref[...], 0),
            axis=1,
            keepdims=True,
        )
        q = jnp.concatenate([q_ref[b][:, g * width : (g + 1) * width] for g in range(heads)], axis=0)
        seen = jnp.concatenate([tree_ref[request]] * heads, axis=0) > 0
        fresh = jnp.where(seen, rows_dot(q, nk_ref[b]) * scale, -1e30)
        position = lax.broadcasted_iota(jnp.int32, (q.shape[0], chunk), 1)
        top = jnp.full((q.shape[0], chunk), -1e30, F32)
        loads[b][0].wait()
        for first in range(0, entries, chunk):
            part = slice(first, first + chunk)
            scores = rows_dot(q, k_ref[b, part, :]) * scale
            scores = jnp.where(position < length - first, scores, -1e30)
            score_ref[:, part] = scores
            top = jnp.maximum(top, scores)
        peak = jnp.maximum(
            jnp.max(top, axis=1, keepdims=True), jnp.max(fresh, axis=1, keepdims=True)
        )
        fresh = jnp.exp(fresh - peak)
        mixed = jnp.dot(fresh.astype(BF16), nv_ref[b], preferred_element_type=F32)
        total = jnp.zeros((q.shape[0], chunk), F32)
        loads[b][1].wait()
        for first in range(0, entries, chunk):
            part = slice(first, first + chunk)
            weights = jnp.exp(score_ref[:, part] - peak)
            total = total + weights
            mixed = mixed + jnp.dot(
                weights.astype(BF16), v_ref[b, part, :], preferred_element_type=F32
            )
        denom = jnp.sum(total, axis=1, keepdims=True) + jnp.sum(fresh, axis=1, keepdims=True)
        attn = (mixed / denom).astype(BF16)
        for g in range(heads):
            out_ref[b * drafts : (b + 1) * drafts, g * width : (g + 1) * width] = attn[
                g * drafts : (g + 1) * drafts
            ]


def attend(axis, queries, key_cache, value_cache, new_keys, new_values, tree_mask, cache_len):
    blocks, drafts, wide = queries.shape
    entries, width = key_cache.shape[1:]
    chunk = 256 if entries % 256 == 0 else entries
    heads = wide // width
    small = (queries, new_keys, new_values, tree_mask, cache_len.reshape(1, -1))
    return pl.pallas_call(
        functools.partial(attend_kernel, axis=axis, heads=heads, chunk=chunk),
        in_specs=[pl.BlockSpec(memory_space=pltpu.HBM)] * 7,
        out_specs=IN_VMEM,
        out_shape=pltpu.VMEM((blocks * drafts, wide), BF16),
        scratch_shapes=[
            *(pltpu.VMEM(x.shape, x.dtype) for x in small),
            pltpu.VMEM(key_cache.shape, BF16),
            pltpu.VMEM(value_cache.shape, BF16),
            pltpu.VMEM((heads * drafts, entries), F32),
            pltpu.SemaphoreType.DMA((len(small),)),
            pltpu.SemaphoreType.DMA((2, blocks)),
        ],
        compiler_params=pltpu.CompilerParams(
            vmem_limit_bytes=MIB + entries * 4 * (blocks * width + heads * drafts)
        ),
        name="attend",
    )(
        *map(in_hbm, (*small, key_cache, value_cache)),
    )


def packing(rows, cols):
    full, rest = divmod(cols, LANES)
    fold = LANES // rest if rest and LANES % rest == 0 and rows % (16 * (LANES // rest)) == 0 else 1
    high = rows // fold if rest else 0
    gain_at = full * rows + high
    return full, rest, fold, high, gain_at, gain_at + -(-(full + (rest > 0)) // 8) * 8


def project_kernel(near_ref, far_ref, w_ref, res_ref, gain_ref, out_ref, x_ref, *, axis, per_head):
    half, high, width = near_ref.shape
    size = 2 * half
    mine = traced_reversed_bits(lax.axis_index(axis), size)
    for t in range(size):
        row = (t % per_head) * high
        col = (t // per_head) * width
        x_ref[row : row + high, col : col + width] = block_of(near_ref, far_ref, mine, t)
    mixed = rows_dot(x_ref[...], w_ref[...])
    rows, cols = res_ref.shape
    stream = (res_ref[...].astype(F32) + mixed).astype(BF16)
    full, rest, fold, high, gain_at, total = packing(rows, cols)
    for i in range(full):
        out_ref[i * rows : (i + 1) * rows, :] = stream[:, i * LANES : (i + 1) * LANES]
    if rest:
        narrow = stream[:, full * LANES :]
        parts = [narrow[q * high : (q + 1) * high] for q in range(fold)]
        if fold * rest < LANES:
            parts.append(jnp.zeros((high, LANES - fold * rest), BF16))
        out_ref[full * rows : gain_at, :] = jnp.concatenate(parts, axis=1)
    gain = jnp.concatenate(
        [gain_ref[...].astype(F32).reshape(1, cols), jnp.zeros((1, (total - gain_at) * LANES - cols), F32)], axis=1
    )
    out_ref[gain_at:, :] = jnp.concatenate(
        [gain[:, i * LANES : (i + 1) * LANES] for i in range(total - gain_at)], axis=0
    ).astype(BF16)


def project(axis, near, far, out_proj_t, residual, gain, per_head):
    rows, cols = residual.shape
    return pl.pallas_call(
        functools.partial(project_kernel, axis=axis, per_head=per_head),
        in_specs=[IN_VMEM] * 5,
        out_specs=IN_VMEM,
        out_shape=pltpu.VMEM((packing(rows, cols)[-1], LANES), BF16),
        scratch_shapes=[pltpu.VMEM((rows, out_proj_t.shape[1]), BF16)],
        compiler_params=pltpu.CompilerParams(vmem_limit_bytes=MIB + 4 * rows * out_proj_t.shape[1]),
        cost_estimate=HINT,
        name="project",
    )(near, far, out_proj_t, residual, gain)


def feed_kernel(near_ref, far_ref, gate_ref, up_ref, down_ref, keep_ref, send_ref, x_ref, h_ref, mine_ref, gain_ref, *, axis, rows, tile, own):
    size = 2 * near_ref.shape[0]
    units, width = down_ref.shape
    cols = width // size
    full, rest, fold, high, gain_at, _ = packing(rows, cols)
    me = lax.axis_index(axis)
    mine = traced_reversed_bits(me, size)
    squares = jnp.zeros((rows, cols), F32)
    for t in range(size):
        block = block_of(near_ref, far_ref, mine, t)
        pieces = [block[i * rows : (i + 1) * rows] for i in range(full)]
        gains = [block[gain_at + i : gain_at + i + 1].astype(F32) for i in range(full)]
        if rest:
            narrow = block[full * rows : gain_at]
            pieces.append(
                jnp.concatenate([narrow[:, q * rest : (q + 1) * rest] for q in range(fold)], axis=0)
            )
            gains.append(block[gain_at + full : gain_at + full + 1, :rest].astype(F32))
        stream = jnp.concatenate(pieces, axis=1)
        part = slice(t * cols, (t + 1) * cols)
        x_ref[:, part] = stream
        gain_ref[:, part] = jnp.concatenate(gains, axis=1)
        wide = stream.astype(F32)
        squares = squares + wide * wide
    inverse = lax.rsqrt(jnp.sum(squares, axis=1, keepdims=True) / width + 1e-06)
    at = lambda shape, dim: lax.broadcasted_iota(jnp.int32, shape, dim)
    device = me ^ traced_reversed_bits(lax.div(at((rows, rows), 0), own), size)
    order = (at((rows, rows), 1) == device * own + lax.rem(at((rows, rows), 0), own)).astype(BF16)
    for first in range(0, width, SPAN):
        part = slice(first, min(first + SPAN, width))
        stream = x_ref[:, part]
        mine_ref[:, part] = jnp.dot(order[: mine_ref.shape[0]], stream, preferred_element_type=F32)
        x_ref[:, part] = (stream.astype(F32) * inverse * gain_ref[:, part]).astype(BF16)
    for first in range(0, units, tile):
        part = slice(first, min(first + tile, units))
        gate = rows_dot(gate_ref[part, :], x_ref[...])
        up = rows_dot(up_ref[part, :], x_ref[...])
        hidden = (gate * jax.nn.sigmoid(gate) * up).astype(BF16)
        h_ref[:, part] = rows_dot(order, hidden).astype(BF16)
    top = rows // 2
    for first in range(0, width, SPAN):
        part = slice(first, min(first + SPAN, width))
        term = jnp.dot(h_ref[...], down_ref[:, part], preferred_element_type=F32)
        keep_ref[:own, part] = term[:own] + mine_ref[:own, part]
        keep_ref[own:, part] = term[own:top]
        send_ref[:, part] = term[top:].astype(BF16)


def feed(axis, near, far, gate_t, up_t, down_w, rows, own):
    units, width = down_w.shape
    tile = 576 if units % 576 == 0 else units
    top = min(rows, -(-own // 16) * 16)
    kept = 2 * (rows * width + rows * units) + 4 * top * width
    return pl.pallas_call(
        functools.partial(feed_kernel, axis=axis, rows=rows, tile=tile, own=own),
        in_specs=[IN_VMEM] * 5,
        out_specs=[IN_VMEM] * 2,
        out_shape=[pltpu.VMEM((rows // 2, width), F32), pltpu.VMEM((rows // 2, width), BF16)],
        scratch_shapes=[
            pltpu.VMEM((rows, width), BF16),
            pltpu.VMEM((rows, units), BF16),
            pltpu.VMEM((top, width), F32),
            pltpu.VMEM((1, width), F32),
        ],
        compiler_params=pltpu.CompilerParams(vmem_limit_bytes=8 * MIB + kept + 44 * (rows - min(rows, 64)) * SPAN),
        name="feed",
    )(resident(near), resident(far), gate_t, up_t, resident(down_w))


def on_device(
    size,
    residual_in,
    queries,
    key_cache,
    value_cache,
    new_keys,
    new_values,
    cache_len,
    tree_mask,
    out_proj,
    norm_gain,
    gate_w,
    up_w,
    down_w,
):
    blocks = queries.shape[0]
    requests = cache_len.shape[0]
    rows, cols = residual_in.shape
    own = rows // size
    gain = norm_gain
    attn = attend(
        "shard", queries, key_cache, value_cache, new_keys, new_values, tree_mask, cache_len
    )
    attn, out_proj = lax.optimization_barrier((attn, out_proj))
    near, far = gather(attn, size, HINT)
    payload = project(
        "shard",
        near,
        far,
        resident(out_proj.T),
        resident(residual_in),
        resident(gain),
        requests // blocks,
    )
    near, far = gather(payload, size)
    keep, send = feed("shard", near, far, resident(gate_w.T), resident(up_w.T), down_w, rows, own)
    bit = 1
    while 4 * own < keep.shape[0] or size <= 4:
        keep = keep + swap(send, bit, size).astype(F32)
        bit *= 2
        if bit == size:
            return keep.astype(BF16)
        half = keep.shape[0] // 2
        keep, send = keep[:half], keep[half:].astype(BF16)
    keep = keep + swap(send, bit, size).astype(F32)
    low, high = size // 4, size // 2
    both = swap(keep[3 * own :].astype(BF16), low + high, size)
    far = swap(keep[own : 2 * own].astype(BF16), high, size)
    near = swap(keep[2 * own : 3 * own].astype(BF16), low, size)
    return (keep[:own] + both.astype(F32) + far.astype(F32) + near.astype(F32)).astype(BF16)


def solution(mesh):
    placed = (
        P("groups", "shard"),
        P(("groups", "shard"), None, None),
        P(("groups", "shard"), None, None),
        P(("groups", "shard"), None, None),
        P(("groups", "shard"), None, None),
        P(("groups", "shard"), None, None),
        P("groups"),
        P("groups", None, None),
        P(None, "shard"),
        P("shard"),
        P(None, "shard"),
        P(None, "shard"),
        P("shard", None),
    )
    return jax.shard_map(
        functools.partial(on_device, mesh.shape["shard"]),
        mesh=mesh,
        in_specs=placed,
        out_specs=P(("groups", "shard"), None),
        check_vma=False,
    )
```
